128 devices in a mesh: stem: 8 (over y_hi, z), leaf: 8 (over x, y_lo), slab: 2 (over core).
Axes of the slice: x: 4, y: 4 (y_hi: 2, y_lo: 2; y = y_hi * 2 + y_lo), z: 4, core: 2. Of those that a mesh axis runs over, the one named last changes fastest.
Arguments:
- branch_rows: bfloat16 [131072, 2, 256], P(('stem', 'leaf', 'slab')), may hold values from -6 to 6
- first_parent: int32 [131072, 1], P(('stem', 'leaf', 'slab')), may hold values from 0 to 15; in each aligned block of 1024 rows (0 to 1023, 1024 to 2047, ...) at most 160 rows name the same one
- second_parent: int32 [131072, 1], P(('stem', 'leaf', 'slab')), may hold values from 0 to 15; in each aligned block of 1024 rows (0 to 1023, 1024 to 2047, ...) at most 160 rows name the same one
- node_first: bfloat16 [16, 2, 256, 256], P(('leaf', 'slab')), may hold values from -1.25 to 1.25
- node_second: bfloat16 [16, 2, 256, 256], P(('leaf', 'slab')), may hold values from -1.25 to 1.25
- stem_tensors: bfloat16 [8, 2, 2, 256, 256], P('stem', None, None, 'slab'), may hold values from -1.25 to 1.25
Outputs:
- amplitudes: bfloat16 [131072, 2, 256], P(('stem', 'leaf', 'slab'))
The draws below stay inside these ranges and needn't reach their ends.
Inputs may be any that keep to these rules, and one draw needn't show every extreme that they name: `first_parent`: within the rows of one device no node is named by more than 160 rows, a bound that some block reaches of them. `second_parent`: within the rows of one device no node is named by more than 160 rows, a bound that some block reaches of them.
All inputs are finite; a program needn't handle non-finite values.
Results may differ from the reference program's by a relative error of at most 0.012.
Values may be sent and summed in bfloat16 or wider, within the bound.
No kernel may reach another device: no remote copies, remote signals or barrier semaphores. Data moves between devices by JAX's collectives and lax.ppermute only.
A program may use at most 64 MiB of HBM per device.

```python
import math
import jax
import jax.numpy as jnp
import numpy as np
from jax import lax

BOND = 256
DEPTH = 2
ROWS_DEV = 1024
CAP = 160
NODES = 16
GROUPS = 8
ROWS = 131072
N_STEM = 8


def tensor_draw(key, lead_shape, salt):
    key = jax.random.fold_in(key, salt)
    angle_key, noise_key = jax.random.split(key)
    spread = 0.35
    factor = 1.0 / math.sqrt(1.0 + spread * spread)
    width = spread / math.sqrt(2.0 * BOND)
    full_shape = lead_shape + (2, BOND, BOND)
    angles = jax.random.uniform(angle_key, lead_shape + (BOND,), jnp.float32, -math.pi, math.pi)
    noise = jnp.clip(jax.random.normal(noise_key, full_shape, jnp.float32), -6.0, 6.0)
    identity = (jnp.arange(BOND)[:, None] == jnp.arange(BOND)[None, :]).astype(jnp.float32)
    diag_real = jnp.cos(angles)[..., :, None] * identity
    diag_imag = jnp.sin(angles)[..., :, None] * identity
    diagonal_part = jnp.stack([diag_real, diag_imag], axis=-3)
    return (factor * (diagonal_part + width * noise)).astype(jnp.float32)


def draw_node_first(key, part):
    return tensor_draw(key, (NODES,), 101).astype(jnp.bfloat16)


def draw_node_second(key, part):
    return tensor_draw(key, (NODES,), 202).astype(jnp.bfloat16)


def draw_stem_tensors(key, part):
    return tensor_draw(key, (GROUPS, DEPTH), 303).astype(jnp.bfloat16)


def shard_levels(rng, dims, pieces, smallest, largest):
    def one(position, blocks):
        steps = jax.random.uniform(jax.random.fold_in(jax.random.fold_in(rng, 6), position), (blocks,), jnp.float32, smallest / len(pieces), largest / len(pieces))
        return jnp.repeat(jnp.exp(steps), dims[position] // blocks).reshape((-1,) + (1,) * (len(dims) - position - 1))

    level = one(*pieces[0])
    for cut in pieces[1:]:
        level = level * one(*cut)
    return level


def deal_out(own_key, own, number, rows, number_of, top, reach, skew):
    order = jax.random.permutation(own_key, number_of)
    packed, common = portions_of(number_of, rows * top, reach, skew, True), portions_of(number_of, rows * top, reach, skew, False)
    places = jnp.arange(number_of)

    def named(sizes, offset_by):
        used = int((sizes > 0).sum())
        fixed = max(1, used // 4)
        moved = fixed + (places - fixed + offset_by * (used - fixed)) % max(1, number_of - fixed)
        return jnp.zeros((number_of,), jnp.int32).at[order[jnp.where(places < fixed, places, moved)]].set(jnp.asarray(sizes, jnp.int32))

    sizes = jnp.where(number % 4 == 0, named(packed, number // 4), named(common, number - number // 4 - 1))
    mixed = jax.random.permutation(jax.random.fold_in(own, 3), number_of)
    source_of, receiver = mixed[0:number_of // 2 * 2:2], mixed[1:number_of // 2 * 2:2]
    margin = jnp.minimum(sizes[source_of] - 1, reach - sizes[receiver]) // 2
    margin = jnp.where((source_of == order[0]) | (receiver == order[0]) | (sizes[receiver] == 0), 0, jnp.maximum(margin, 0))
    moved = jax.random.randint(jax.random.fold_in(own, 4), (number_of // 2,), 0, 1 << 20) % (margin + 1)
    sizes = sizes.at[source_of].add(-moved).at[receiver].add(moved)
    labels = jnp.searchsorted(jnp.cumsum(sizes), jnp.arange(rows * top), side="right").astype(jnp.int32)
    table = labels.reshape(top, rows).T
    table = table[jax.random.permutation(jax.random.fold_in(own, 1), rows)]
    offset_by = jax.random.randint(jax.random.fold_in(own, 2), (rows, 1), 0, top)
    return jnp.take_along_axis(table, (jnp.arange(top)[None, :] + offset_by) % top, axis=1)


def portions_of(number_of, total, most, lean, full):
    loads = [(1 << 20) // math.isqrt(grade ** lean) + 1 for grade in range(1, number_of + 1)]
    largest = most if full else min(most, max(-(-total // number_of), total * loads[0] // sum(loads)))
    least = 1 if total - largest >= number_of - 1 else 0
    given, spare = [largest] + [least] * (number_of - 1), total - largest - least * (number_of - 1)
    while spare > 0:
        movable = [i for i in range(1, number_of) if given[i] < largest] or [i for i in range(1, number_of) if given[i] < most]
        mass, remaining = sum([loads[i] for i in movable]), spare
        for i in movable:
            extra = min(most - given[i], max(1, remaining * loads[i] // mass), spare)
            given[i] = given[i] + extra
            spare = spare - extra
    return np.array(given)


def scatter_about(stream_key, extent, scale, limit, cuts=(), kind=jnp.bfloat16):
    entries = jax.random.normal(stream_key, extent, jnp.float32) * scale
    if len(cuts) > 0:
        entries = shard_levels(stream_key, extent, cuts, -0.22, 0.18) * entries
    return jnp.clip(entries, min=-limit, max=limit).astype(kind)


def setup_inputs(seed: int = 0) -> dict:
    key_of = jax.random.split(jax.random.key(seed), 7)
    branch_rows = scatter_about(key_of[0], (ROWS, 2, BOND), 1.0, 6.0, ((0, 128),))
    first_parent_keys = jax.random.split(jax.random.fold_in(key_of[1], 1), ROWS // ROWS_DEV)
    first_parent_turns = jax.random.permutation(jax.random.fold_in(key_of[1], 3), ROWS // ROWS_DEV)
    first_parent = jax.vmap(lambda own, number: deal_out(jax.random.fold_in(key_of[1], 2), own, number, ROWS_DEV, NODES, 1, CAP, 2))(first_parent_keys, first_parent_turns).reshape((ROWS, 1))
    second_parent_keys = jax.random.split(jax.random.fold_in(key_of[2], 1), ROWS // ROWS_DEV)
    second_parent_turns = jax.random.permutation(jax.random.fold_in(key_of[2], 3), ROWS // ROWS_DEV)
    second_parent = jax.vmap(lambda own, number: deal_out(jax.random.fold_in(key_of[2], 2), own, number, ROWS_DEV, NODES, 1, CAP, 2))(second_parent_keys, second_parent_turns).reshape((ROWS, 1))
    node_first = draw_node_first(jax.random.fold_in(key_of[6], 71), 0)
    node_second = draw_node_second(jax.random.fold_in(key_of[6], 71), 0)
    stem_tensors = draw_stem_tensors(jax.random.fold_in(key_of[6], 71), 0)
    return {"branch_rows": branch_rows, "first_parent": first_parent, "second_parent": second_parent, "node_first": node_first, "node_second": node_second, "stem_tensors": stem_tensors}


def complex_plain(row_block, matrix):
    values = row_block.astype(jnp.float32)
    weights = matrix.astype(jnp.float32)
    real_part = jnp.dot(values[:, 0], weights[0]) - jnp.dot(values[:, 1], weights[1])
    imag_part = jnp.dot(values[:, 0], weights[1]) + jnp.dot(values[:, 1], weights[0])
    return jnp.stack([real_part, imag_part], axis=1).astype(jnp.bfloat16)


def group_apply(current, matrix):
    values = current.astype(jnp.float32)
    weights = matrix.astype(jnp.float32)
    real_part = jnp.einsum('grb,gbe->gre', values[:, :, 0], weights[:, 0]) - jnp.einsum('grb,gbe->gre', values[:, :, 1], weights[:, 1])
    imag_part = jnp.einsum('grb,gbe->gre', values[:, :, 0], weights[:, 1]) + jnp.einsum('grb,gbe->gre', values[:, :, 1], weights[:, 0])
    return jnp.stack([real_part, imag_part], axis=2).astype(jnp.bfloat16)


def node_level(row_block, parent, tensors):
    targets = parent[:, 0].astype(jnp.int32)
    row_total = targets.shape[0]
    ordering = jnp.argsort(targets, stable=True).astype(jnp.int32)
    sorted_targets = targets[ordering]
    matches = (targets[:, None] == jnp.arange(NODES, dtype=jnp.int32)[None, :]).astype(jnp.int32)
    node_sizes = jnp.sum(matches, axis=0).astype(jnp.int32)
    node_starts = (jnp.cumsum(node_sizes) - node_sizes).astype(jnp.int32)
    placement = (jnp.arange(row_total, dtype=jnp.int32) - node_starts[sorted_targets]).astype(jnp.int32)
    buffer_len = min(row_total, CAP * N_STEM * NODES)
    buffered = jnp.zeros((NODES, buffer_len, 2, BOND), jnp.bfloat16)
    buffered = buffered.at[sorted_targets, placement].set(row_block[ordering])
    finished = lax.map(lambda pair: complex_plain(pair[0], pair[1]), (buffered, tensors))
    sorted_out = finished[sorted_targets, placement]
    return jnp.zeros_like(row_block).at[ordering].set(sorted_out)


def reference(branch_rows, first_parent, second_parent, node_first, node_second, stem_tensors):
    first = node_level(branch_rows, first_parent, node_first)
    second = node_level(first, second_parent, node_second)
    current = second.reshape(N_STEM, -1, 2, BOND)
    for visit in range(N_STEM):
        turned = jnp.roll(stem_tensors, -visit, axis=0)
        for layer_index in range(DEPTH):
            current = group_apply(current, turned[:, layer_index])
    return current.reshape(-1, 2, BOND)
```

```python
import jax
import jax.numpy as jnp
from jax import lax
from jax.experimental import pallas as pl
from jax.experimental.pallas import tpu as pltpu
from jax.sharding import PartitionSpec as P

AXES = ("stem", "leaf", "slab")
ROWS = 1024
BOND = 256
NODES = 16
PAD = 16
SORTED = 1280
WINDOW = 80
ROOM = SORTED + 2 * WINDOW
F32 = jnp.float32
BF16 = jnp.bfloat16


def device_index(x, y, z, c):
    return (((y // 2) * 4 + z) * 8 + (x * 2 + y % 2)) * 2 + c


def routed(value, move):
    pairs = []
    for x in range(4):
        for y in range(4):
            for z in range(4):
                for c in range(2):
                    tx, ty, tz, tc = move(x, y, z, c)
                    pairs.append((device_index(x, y, z, c), device_index(tx % 4, ty % 4, tz % 4, tc)))
    return lax.ppermute(value, AXES, pairs)


def swap(value):
    return routed(value, lambda x, y, z, c: (x, y, z, 1 - c))


def along_x(value):
    return routed(value, lambda x, y, z, c: (x + 1 - 2 * c, y, z, c))


def along_y(value):
    return routed(value, lambda x, y, z, c: (x, y + 1 - 2 * c, z, c))


def along_z(value):
    return routed(value, lambda x, y, z, c: (x, y, z + 1 - 2 * c, c))


def across_z(value):
    return routed(value, lambda x, y, z, c: (x, y, z + 2, c))


def across_y(value):
    return routed(value, lambda x, y, z, c: (x, y + 2, z, c))


def mm(a, b):
    return jnp.dot(a, b, preferred_element_type=F32)


def complex_mm(ar, ai, br, bi):
    return mm(ar, br) - mm(ai, bi), mm(ar, bi) + mm(ai, br)


def slot_of(parent, x, p, c):
    dx = (parent // 4 - x + 4) % 4
    dp = ((parent // 2) % 2 + p) % 2
    dc = (parent % 2 + c) % 2
    near = dx == 3 - 2 * c
    side = jnp.where(near, jnp.where(dc == 0, 2, 6), jnp.where(dc == 0, 7, 3))
    side = side + 6 * dp
    base = jnp.where(dx == 0, dc + 4 * dp, 10 + dc + 4 * dp)
    return jnp.where((dx == 1) | (dx == 3), side, base)


def positions(key, triangle):
    node = lax.broadcasted_iota(jnp.int32, (NODES, ROWS), 0)
    match = node == key
    match_f = match.astype(F32)
    before = mm(match.astype(BF16), triangle)
    count = jnp.sum(match_f, axis=1, keepdims=True)
    padded = jnp.floor((count + (PAD - 1)) * (1.0 / PAD)) * PAD
    lower = (
        lax.broadcasted_iota(jnp.int32, (NODES, NODES), 1) < lax.broadcasted_iota(jnp.int32, (NODES, NODES), 0)
    ).astype(BF16)
    start = mm(lower, jnp.broadcast_to(padded, (NODES, 128)).astype(BF16))
    place = jnp.sum(match_f * (start[:, :1] + before), axis=0, keepdims=True)
    return place, start, count


def prepare_kernel(key1_ref, key2_ref, rows_ref, x1_ref, q_ref, col_ref, table_ref, sel):
    lane = lax.broadcasted_iota(jnp.int32, (ROWS, ROWS), 1)
    sub = lax.broadcasted_iota(jnp.int32, (ROWS, ROWS), 0)
    triangle = (sub < lane).astype(BF16)
    place1, start1, count1 = positions(key1_ref[...], triangle)
    place2, start2, count2 = positions(key2_ref[...], triangle)
    table_ref[0] = start1.astype(jnp.int32)
    table_ref[1] = jnp.broadcast_to(count1, (NODES, 128)).astype(jnp.int32)
    table_ref[2] = start2.astype(jnp.int32)
    table_ref[3] = jnp.broadcast_to(count2, (NODES, 128)).astype(jnp.int32)
    place1_i = place1.astype(jnp.int32)
    step = 256
    for block in range(SORTED // step):
        spot = lax.broadcasted_iota(jnp.int32, (step, ROWS), 0) + block * step
        one_hot = (spot == place1_i).astype(BF16)
        sel[pl.ds(block * step, step), :] = one_hot
        x1_ref[pl.ds(block * step, step), :] = mm(one_hot, rows_ref[...]).astype(BF16)
    x1_ref[pl.ds(SORTED, ROOM - SORTED), :] = jnp.zeros((ROOM - SORTED, 2 * BOND), BF16)
    high = jnp.floor(place2 * (1.0 / 64.0))
    low = place2 - 64.0 * high
    which = lax.broadcasted_iota(jnp.int32, (8, ROWS), 0)
    parts = jnp.where(which == 0, high + 1.0, jnp.where(which == 1, low, 0.0)).astype(BF16)
    found = lax.dot_general(parts, sel[...], (((1,), (1,)), ((), ())), preferred_element_type=F32)
    q = (found[0:1] - 1.0) * 64.0 + found[1:2]
    q_ref[...] = jnp.broadcast_to(q, (8, SORTED)).astype(jnp.int32)
    col = jnp.transpose(jnp.broadcast_to(place2, (128, ROWS)))
    col_ref[...] = col.astype(jnp.int32)


def level(x_ref, out_ref, table_ref, row, slots, which):
    for k, slot in enumerate(slots):
        begin = pl.multiple_of(table_ref[row, k, 0], PAD)
        count = table_ref[row + 1, k, 0]
        for part in range(2):
            @pl.when(count > part * WINDOW)
            def _(begin=begin, part=part, slot=slot):
                spot = pl.ds(pl.multiple_of(begin + part * WINDOW, PAD), WINDOW)
                re, im = complex_mm(
                    x_ref[spot, :BOND], x_ref[spot, BOND:], slot[which, 0], slot[which, 1]
                )
                out_ref[spot, :BOND] = re.astype(BF16)
                out_ref[spot, BOND:] = im.astype(BF16)


def rows_kernel(*refs):
    table_ref, x1_ref, q_ref, col_ref, m_ref = refs[:5]
    slots = refs[5 : 5 + NODES]
    out_ref, first, x2, second = refs[5 + NODES :]
    first[...] = jnp.zeros_like(first)
    second[...] = jnp.zeros_like(second)
    x2[pl.ds(SORTED, ROOM - SORTED), :] = jnp.zeros((ROOM - SORTED, 2 * BOND), BF16)
    level(x1_ref, first, table_ref, 0, slots, 0)
    step = 256
    for block in range(SORTED // step):
        spot = lax.broadcasted_iota(jnp.int32, (step, SORTED), 0) + block * step
        one_hot = (spot == q_ref[0:1, :]).astype(BF16)
        x2[pl.ds(block * step, step), :] = mm(one_hot, first[pl.ds(0, SORTED), :]).astype(BF16)
    level(x2, second, table_ref, 2, slots, 1)
    for block in range(ROWS // step):
        spot = pl.ds(block * step, step)
        lane = lax.broadcasted_iota(jnp.int32, (step, SORTED), 1)
        one_hot = (lane == col_ref[spot, 0:1]).astype(BF16)
        picked = mm(one_hot, second[pl.ds(0, SORTED), :]).astype(BF16)
        re, im = complex_mm(picked[:, :BOND], picked[:, BOND:], m_ref[0], m_ref[1])
        out_ref[0, spot, :] = re.astype(BF16)
        out_ref[1, spot, :] = im.astype(BF16)


def pair_kernel(where_ref, own_ref, other_ref, p_ref, full):
    c = where_ref[1]
    for layer in range(2):
        for part in range(2):
            full[layer, part, pl.ds(pl.multiple_of(c * 128, 128), 128), :] = own_ref[layer, part]
            full[layer, part, pl.ds(pl.multiple_of((1 - c) * 128, 128), 128), :] = other_ref[layer, part]
    re, im = complex_mm(full[0, 0], full[0, 1], full[1, 0], full[1, 1])
    p_ref[0] = re.astype(BF16)
    p_ref[1] = im.astype(BF16)


def gather_ring(where_ref, refs, held):
    z, c = where_ref[0], where_ref[1]
    spots = (z, (z + 3 + 2 * c) % 4, (z + 1 + 2 - 2 * c + 2) % 4, (z + 2) % 4)
    for spot, ref in zip(spots, refs):
        held[spot] = ref[...]


def chain(held, order, out_ref):
    re, im = held[order[0], 0], held[order[0], 1]
    for spot in order[1:]:
        re, im = complex_mm(re, im, held[spot, 0], held[spot, 1])
        re, im = re.astype(BF16), im.astype(BF16)
    out_ref[0] = re
    out_ref[1] = im


def ring_kernel(where_ref, a_ref, b_ref, c_ref, d_ref, t_ref, held):
    gather_ring(where_ref, (a_ref, b_ref, c_ref, d_ref), held)
    chain(held, (0, 1, 2, 3), t_ref)


def loop_kernel(where_ref, a_ref, b_ref, c_ref, d_ref, far_ref, m_ref, held):
    gather_ring(where_ref, (a_ref, b_ref, c_ref, d_ref), held)
    held[4] = far_ref[...]
    z = where_ref[0]
    chain(held, tuple((z + i) % 5 for i in range(5)), m_ref)


def vmem():
    return pl.BlockSpec(memory_space=pltpu.VMEM)


def smem():
    return pl.BlockSpec(memory_space=pltpu.SMEM)


def call(kernel, out, ins, scratch, flops, moved):
    return pl.pallas_call(
        kernel,
        out_shape=out,
        in_specs=ins,
        out_specs=jax.tree.map(lambda _: vmem(), out),
        scratch_shapes=scratch,
        cost_estimate=pl.CostEstimate(flops=flops, bytes_accessed=moved, transcendentals=0),
        compiler_params=pltpu.CompilerParams(vmem_limit_bytes=40 * 2**20),
    )


def body(branch_rows, first_parent, second_parent, node_first, node_second, stem_tensors):
    stem, leaf, core = (lax.axis_index(name) for name in AXES)
    x, p, z = leaf // 2, leaf % 2, stem % 4
    where = jnp.stack([z, core]).astype(jnp.int32)
    matrix = jax.ShapeDtypeStruct((2, BOND, BOND), BF16)

    own = jnp.concatenate([node_first, node_second], axis=0)
    side = along_x(own)
    sibling = swap(own)
    stem_own = stem_tensors[0]
    stem_other = swap(stem_own)
    own_later, sibling, stem_other = lax.optimization_barrier((own, sibling, stem_other))
    side_far = along_x(sibling)
    turned = along_y(own_later)

    product = call(pair_kernel, matrix, [smem(), vmem(), vmem()],
                   [pltpu.VMEM((2, 2, BOND, BOND), BF16)], 2**28, 2**20)(where, stem_own, stem_other)

    rows = branch_rows.reshape(ROWS, 2 * BOND)
    key1 = slot_of(first_parent.reshape(1, ROWS), x, p, core)
    key2 = slot_of(second_parent.reshape(1, ROWS), x, p, core)
    x1, q, col, table = call(
        prepare_kernel,
        (
            jax.ShapeDtypeStruct((ROOM, 2 * BOND), BF16),
            jax.ShapeDtypeStruct((8, SORTED), jnp.int32),
            jax.ShapeDtypeStruct((ROWS, 128), jnp.int32),
            jax.ShapeDtypeStruct((4, NODES, 128), jnp.int32),
        ),
        [vmem(), vmem(), vmem()],
        [pltpu.VMEM((SORTED, ROWS), BF16)],
        2**31, 2**22,
    )(key1, key2, rows)

    near = along_z(product)
    opposite = across_z(product)
    near_other = swap(near)
    ring = (product, near, near_other, opposite)
    total = call(ring_kernel, matrix, [smem()] + [vmem()] * 4,
                 [pltpu.VMEM((4, 2, BOND, BOND), BF16)], 2**29, 2**20)(where, *ring)
    far = across_y(total)
    loop = call(loop_kernel, matrix, [smem()] + [vmem()] * 5,
                [pltpu.VMEM((5, 2, BOND, BOND), BF16)], 2**29, 2**20)(where, *ring, far)

    across = along_x(side)
    side_turned = along_y(side)
    side_far_turned = along_y(side_far)
    across_turned = along_y(across)
    slots = [own, sibling]
    for value in (side, turned, side_far, side_turned, across, side_far_turned, across_turned):
        slots += [value, swap(value)]

    out = call(
        rows_kernel,
        jax.ShapeDtypeStruct((2, ROWS, BOND), BF16),
        [smem()] + [vmem()] * (4 + NODES),
        [pltpu.VMEM((ROOM, 2 * BOND), BF16)] * 3,
        2**33, 2**24,
    )(table, x1, q, col, loop, *slots)
    return jnp.transpose(out, (1, 0, 2))


def solution(mesh):
    return jax.shard_map(
        body,
        mesh=mesh,
        in_specs=(
            P(AXES, None, None),
            P(AXES, None),
            P(AXES, None),
            P(("leaf", "slab"), None, None, None),
            P(("leaf", "slab"), None, None, None),
            P("stem", None, None, "slab", None),
        ),
        out_specs=P(AXES, None, None),
        check_vma=False,
    )
```

```python
import jax
import jax.numpy as jnp
from jax import lax
from jax.experimental import pallas as pl
from jax.experimental.pallas import tpu as pltpu
from jax.sharding import PartitionSpec as P

AXES = ("stem", "leaf", "slab")
ROWS = 1024
BOND = 256
NODES = 16
PAD = 16
SORTED = 1280
WINDOW = 80
ROOM = SORTED + 2 * WINDOW
TAIL = ROOM - 928
F32 = jnp.float32
BF16 = jnp.bfloat16


def device_index(x, y, z, c):
    return (((y // 2) * 4 + z) * 8 + (x * 2 + y % 2)) * 2 + c


def routed(value, move):
    pairs = []
    for x in range(4):
        for y in range(4):
            for z in range(4):
                for c in range(2):
                    tx, ty, tz, tc = move(x, y, z, c)
                    pairs.append((device_index(x, y, z, c), device_index(tx % 4, ty % 4, tz % 4, tc)))
    return lax.ppermute(value, AXES, pairs)


def swap(value):
    return routed(value, lambda x, y, z, c: (x, y, z, 1 - c))


def along_x(value):
    return routed(value, lambda x, y, z, c: (x + 1 - 2 * c, y, z, c))


def along_y(value):
    return routed(value, lambda x, y, z, c: (x, y + 1 - 2 * c, z, c))


def along_z(value):
    return routed(value, lambda x, y, z, c: (x, y, z + 1 - 2 * c, c))


def across_z(value):
    return routed(value, lambda x, y, z, c: (x, y, z + 2, c))


def across_y(value):
    return routed(value, lambda x, y, z, c: (x, y + 2, z, c))


def mm(a, b):
    return jnp.dot(a, b, preferred_element_type=F32)


def complex_mm(ar, ai, br, bi):
    return mm(ar, br) - mm(ai, bi), mm(ar, bi) + mm(ai, br)


def slot_of(parent, x, p, c):
    dx = (parent // 4 - x + 4) % 4
    dp = ((parent // 2) % 2 + p) % 2
    dc = (parent % 2 + c) % 2
    near = dx == 3 - 2 * c
    side = jnp.where(near, jnp.where(dc == 0, 2, 6), jnp.where(dc == 0, 7, 3))
    side = side + 6 * dp
    base = jnp.where(dx == 0, dc + 4 * dp, 10 + dc + 4 * dp)
    return jnp.where((dx == 1) | (dx == 3), side, base)


def round_up(count):
    return jnp.floor((count + (PAD - 1)) * (1.0 / PAD)) * PAD


def iota(shape, axis):
    return lax.broadcasted_iota(jnp.int32, shape, axis)


def prepare_kernel(
    where_ref, parents_ref, rows_hbm, x1_ref, goes_ref, place_ref, table_ref, sel, rows_ref, sem
):
    copy = pltpu.make_async_copy(rows_hbm, rows_ref, sem)
    copy.start()
    x, p, c = where_ref[2], where_ref[3], where_ref[1]
    triangle = (iota((ROWS, ROWS), 0) < iota((ROWS, ROWS), 1)).astype(BF16)
    node = iota((NODES, ROWS), 0)
    match = jnp.concatenate(
        [
            (node == slot_of(parents_ref[0:1, :], x, p, c)).astype(F32),
            (node == slot_of(parents_ref[1:2, :], x, p, c)).astype(F32),
        ],
        axis=0,
    )
    before = mm(match.astype(BF16), triangle)
    total = round_up(jnp.sum(match, axis=1, keepdims=True))
    lower = (iota((NODES, NODES), 1) < iota((NODES, NODES), 0)).astype(BF16)
    upper = (iota((NODES, NODES), 0) < iota((NODES, NODES), 1)).astype(BF16)
    places, rows_of_table = [], []
    for way in range(2):
        own = match[way * NODES : (way + 1) * NODES]
        padded = jnp.broadcast_to(total[way * NODES : (way + 1) * NODES], (NODES, 128)).astype(BF16)
        start = mm(lower, padded)[:, :1]
        places.append(
            jnp.sum(own * (start + before[way * NODES : (way + 1) * NODES]), axis=0, keepdims=True)
        )
        count = lax.dot_general(
            jnp.ones((8, ROWS), BF16), own.astype(BF16), (((1,), (1,)), ((), ())), preferred_element_type=F32
        )
        rows_of_table += [mm(round_up(count).astype(BF16), upper), count]
    row = iota((8, NODES), 0)
    table = jnp.where(row == 0, rows_of_table[0], 0.0)
    for k in range(1, 4):
        table = jnp.where(row == k, rows_of_table[k], table)
    table_ref[...] = table.astype(jnp.int32)

    place1 = places[0].astype(jnp.int32)
    copy.wait()
    flat = rows_ref[...].reshape(ROWS, 2 * BOND)
    step = 256
    for block in range(SORTED // step):
        spot = pl.ds(block * step, step)
        one_hot = (iota((step, ROWS), 0) + block * step == place1).astype(BF16)
        sel[spot, :] = one_hot
        sorted_rows = mm(one_hot, flat).astype(BF16)
        x1_ref[0, spot, :] = sorted_rows[:, :BOND]
        x1_ref[1, spot, :] = sorted_rows[:, BOND:]
    x1_ref[:, pl.ds(SORTED, ROOM - SORTED), :] = jnp.zeros((2, ROOM - SORTED, BOND), BF16)

    high = jnp.floor(places[1] * (1.0 / 64.0))
    low = places[1] - 64.0 * high
    which = iota((8, ROWS), 0)
    parts = jnp.where(which == 0, high + 1.0, jnp.where(which == 1, low, 0.0)).astype(BF16)
    found = lax.dot_general(parts, sel[...], (((1,), (1,)), ((), ())), preferred_element_type=F32)
    goes_ref[...] = jnp.broadcast_to((found[0:1] - 1.0) * 64.0 + found[1:2], (8, SORTED)).astype(jnp.int32)
    place_ref[...] = jnp.broadcast_to(places[1], (8, ROWS))


def select_kernel(goes_ref, place_ref, to2_ref, back_ref):
    step = 256
    for block in range(SORTED // step):
        to2_ref[pl.ds(block * step, step), :] = (
            iota((step, SORTED), 0) + block * step == goes_ref[0:1, :]
        ).astype(BF16)
    column = jnp.transpose(jnp.broadcast_to(place_ref[0:1, :], (128, ROWS))).astype(jnp.int32)[:, :1]
    for block in range(ROWS // step):
        back_ref[pl.ds(block * step, step), :] = (
            iota((step, SORTED), 1) == column[block * step : (block + 1) * step]
        ).astype(BF16)


def window(x_ref, out_ref, slot, which, begin):
    spot = pl.ds(pl.multiple_of(begin, PAD), WINDOW)
    pair = x_ref[:, spot, :].reshape(2 * WINDOW, BOND)
    by_re, by_im = mm(pair, slot[which, 0]), mm(pair, slot[which, 1])
    out_ref[0, spot, :] = (by_re[:WINDOW] - by_im[WINDOW:]).astype(BF16)
    out_ref[1, spot, :] = (by_im[:WINDOW] + by_re[WINDOW:]).astype(BF16)


def level(x_ref, out_ref, table_ref, row, slots, which):
    out_ref[:, pl.ds(ROOM - TAIL, TAIL), :] = jnp.zeros((2, TAIL, BOND), BF16)
    for k, slot in enumerate(slots):
        @pl.when(table_ref[row + 1, k] > WINDOW)
        def _(k=k, slot=slot):
            window(x_ref, out_ref, slot, which, table_ref[row, k] + WINDOW)
    for k, slot in enumerate(slots):
        window(x_ref, out_ref, slot, which, table_ref[row, k])


def rows_kernel(*refs):
    table_ref, x1_ref, to2_ref, back_ref, m_ref = refs[:5]
    slots = refs[5 : 5 + NODES]
    out_ref, first, x2, second = refs[5 + NODES :]
    level(x1_ref, first, table_ref, 0, slots, 0)
    x2[:, pl.ds(SORTED, ROOM - SORTED), :] = jnp.zeros((2, ROOM - SORTED, BOND), BF16)
    step = 256
    for block in range(SORTED // step):
        spot = pl.ds(block * step, step)
        for part in range(2):
            x2[part, spot, :] = mm(to2_ref[spot, :], first[part, pl.ds(0, SORTED), :]).astype(BF16)
    level(x2, second, table_ref, 2, slots, 1)
    spread = iota((2 * step, 2 * step), 0)
    interleave = (iota((2 * step, 2 * step), 1) == spread // 2 + step * (spread % 2)).astype(BF16)
    for block in range(ROWS // step):
        spot = pl.ds(block * step, step)
        pair = jnp.concatenate(
            [mm(back_ref[spot, :], second[part, pl.ds(0, SORTED), :]).astype(BF16) for part in range(2)], axis=0
        )
        by_re, by_im = mm(pair, m_ref[0]), mm(pair, m_ref[1])
        pair = jnp.concatenate([by_re[:step] - by_im[step:], by_im[:step] + by_re[step:]], axis=0)
        out_ref[spot] = mm(interleave, pair.astype(BF16)).astype(BF16).reshape(step, 2, BOND)


def pair_kernel(where_ref, own_ref, other_ref, p_ref, full):
    c = where_ref[1]
    for layer in range(2):
        for part in range(2):
            full[layer, part, pl.ds(pl.multiple_of(c * 128, 128), 128), :] = own_ref[layer, part]
            full[layer, part, pl.ds(pl.multiple_of((1 - c) * 128, 128), 128), :] = other_ref[layer, part]
    re, im = complex_mm(full[0, 0], full[0, 1], full[1, 0], full[1, 1])
    p_ref[0] = re.astype(BF16)
    p_ref[1] = im.astype(BF16)


def gather_ring(where_ref, refs, held):
    z, c = where_ref[0], where_ref[1]
    spots = (z, (z + 3 + 2 * c) % 4, (z + 1 + 2 - 2 * c + 2) % 4, (z + 2) % 4)
    for spot, ref in zip(spots, refs):
        held[spot] = ref[...]


def half_of(core):
    return pl.ds(pl.multiple_of(core * (BOND // 2), BOND // 2), BOND // 2)


def ring_kernel(where_ref, a_ref, b_ref, c_ref, d_ref, t_ref, held):
    gather_ring(where_ref, (a_ref, b_ref, c_ref, d_ref), held)
    rows = half_of(where_ref[1])
    re, im = held[0, 0, rows, :], held[0, 1, rows, :]
    for spot in (1, 2, 3):
        re, im = complex_mm(re, im, held[spot, 0], held[spot, 1])
        re, im = re.astype(BF16), im.astype(BF16)
    t_ref[0] = re
    t_ref[1] = im


def loop_kernel(where_ref, a_ref, b_ref, c_ref, d_ref, far_ref, far_other_ref, m_ref, held):
    gather_ring(where_ref, (a_ref, b_ref, c_ref, d_ref), held)
    z, core = where_ref[0], where_ref[1]
    for part in range(2):
        held[4, part, half_of(core), :] = far_ref[part]
        held[4, part, half_of(1 - core), :] = far_other_ref[part]
    re, im = held[z, 0], held[z, 1]
    for i in range(1, 5):
        re, im = complex_mm(re, im, held[(z + i) % 5, 0], held[(z + i) % 5, 1])
        re, im = re.astype(BF16), im.astype(BF16)
    m_ref[0] = re
    m_ref[1] = im


def vmem():
    return pl.BlockSpec(memory_space=pltpu.VMEM)


def smem():
    return pl.BlockSpec(memory_space=pltpu.SMEM)


def call(kernel, out, ins, scratch, flops, moved, room=20):
    return pl.pallas_call(
        kernel,
        out_shape=out,
        in_specs=ins,
        out_specs=jax.tree.map(lambda _: vmem(), out),
        scratch_shapes=scratch,
        cost_estimate=pl.CostEstimate(flops=flops, bytes_accessed=moved, transcendentals=0),
        compiler_params=pltpu.CompilerParams(vmem_limit_bytes=room * 2**20),
    )


def after(value, *others):
    return lax.optimization_barrier((value, *others))[0]


def body(branch_rows, first_parent, second_parent, node_first, node_second, stem_tensors):
    stem, leaf, core = (lax.axis_index(name) for name in AXES)
    where = jnp.stack([stem % 4, core, leaf // 2, leaf % 2]).astype(jnp.int32)
    matrix = jax.ShapeDtypeStruct((2, BOND, BOND), BF16)
    half = jax.ShapeDtypeStruct((2, BOND // 2, BOND), BF16)

    own = lax.optimization_barrier(jnp.concatenate([node_first, node_second], axis=0))
    with jax.named_scope("sibling"):
        sibling = swap(own)
    with jax.named_scope("side"):
        side = along_x(own)
    stem_own = stem_tensors[0]
    with jax.named_scope("stem_other"):
        stem_other = swap(stem_own)
    own_later, sibling = lax.optimization_barrier((own, sibling))
    with jax.named_scope("side_far"):
        side_far = along_x(sibling)
    with jax.named_scope("turned"):
        turned = along_y(own_later)

    product = call(pair_kernel, matrix, [smem(), vmem(), vmem()],
                   [pltpu.VMEM((2, 2, BOND, BOND), BF16)], 2**28, 2**20)(after(where, sibling), stem_own, stem_other)
    with jax.named_scope("near"):
        near = along_z(product)
    with jax.named_scope("opposite"):
        opposite = across_z(product)

    hbm = pl.BlockSpec(memory_space=pltpu.HBM)
    parents = jnp.concatenate([first_parent.reshape(1, ROWS), second_parent.reshape(1, ROWS)], axis=0)
    side_later = after(side, product, turned)
    with jax.named_scope("side_turned"):
        side_turned = along_y(side_later)
    with jax.named_scope("across"):
        across = along_x(side_later)
    with jax.named_scope("near_other"):
        near_other = swap(near)
    with jax.named_scope("side_far_turned"):
        side_far_turned = along_y(after(side_far, product))
    ring = (product, near, near_other, opposite)
    total = call(ring_kernel, half, [smem()] + [vmem()] * 4,
                 [pltpu.VMEM((4, 2, BOND, BOND), BF16)], 2**29, 2**20)(where, *ring)
    with jax.named_scope("far"):
        far = across_y(total)
    with jax.named_scope("across_turned"):
        across_turned = along_y(after(across, total))
    x1, goes, place, table = call(
        prepare_kernel,
        (
            jax.ShapeDtypeStruct((2, ROOM, BOND), BF16),
            jax.ShapeDtypeStruct((8, SORTED), jnp.int32),
            jax.ShapeDtypeStruct((8, ROWS), F32),
            jax.ShapeDtypeStruct((8, NODES), jnp.int32),
        ),
        [smem(), vmem(), hbm],
        [
            pltpu.VMEM((SORTED, ROWS), BF16),
            pltpu.VMEM((ROWS, 2, BOND), BF16),
            pltpu.SemaphoreType.DMA,
        ],
        2**31, 2**22,
    )(after(where, across, total), parents, branch_rows)
    to2, back = call(
        select_kernel,
        (jax.ShapeDtypeStruct((SORTED, SORTED), BF16), jax.ShapeDtypeStruct((ROWS, SORTED), BF16)),
        [vmem(), vmem()], [], 2**30, 2**22,
    )(after(goes, side_turned), place)
    with jax.named_scope("far_other"):
        far_other = swap(far)
    loop = call(loop_kernel, matrix, [smem()] + [vmem()] * 6,
                [pltpu.VMEM((5, 2, BOND, BOND), BF16)], 2**29, 2**20)(where, *ring, far, far_other)

    slots = [own, sibling]
    for value in (side, turned, side_far, side_turned, across, side_far_turned, across_turned):
        with jax.named_scope("shared"):
            slots += [value, swap(after(value, to2))]

    return call(
        rows_kernel,
        jax.ShapeDtypeStruct((ROWS, 2, BOND), BF16),
        [smem()] + [vmem()] * (4 + NODES),
        [pltpu.VMEM((2, ROOM, BOND), BF16)] * 3,
        2**33, 2**24,
    )(table, x1, to2, back, loop, *slots)


def solution(mesh):
    return jax.shard_map(
        body,
        mesh=mesh,
        in_specs=(
            P(AXES, None, None),
            P(AXES, None),
            P(AXES, None),
            P(("leaf", "slab"), None, None, None),
            P(("leaf", "slab"), None, None, None),
            P("stem", None, None, "slab", None),
        ),
        out_specs=P(AXES, None, None),
        check_vma=False,
    )
```

```python
import jax
import jax.numpy as jnp
from jax import lax
from jax.experimental import pallas as pl
from jax.experimental.pallas import tpu as pltpu
from jax.sharding import PartitionSpec as P

AXES = ("stem", "leaf", "slab")
ROWS = 1024
BOND = 256
NODES = 16
PAD = 16
SORTED = 1280
WINDOW = 80
ROOM = SORTED + 2 * WINDOW
TAIL = ROOM - 928
F32 = jnp.float32
BF16 = jnp.bfloat16


def device_index(x, y, z, c):
    return (((y // 2) * 4 + z) * 8 + (x * 2 + y % 2)) * 2 + c


def routed(value, move):
    pairs = []
    for x in range(4):
        for y in range(4):
            for z in range(4):
                for c in range(2):
                    tx, ty, tz, tc = move(x, y, z, c)
                    pairs.append((device_index(x, y, z, c), device_index(tx % 4, ty % 4, tz % 4, tc)))
    return lax.ppermute(value, AXES, pairs)


def swap(value):
    return routed(value, lambda x, y, z, c: (x, y, z, 1 - c))


def along_x(value):
    return routed(value, lambda x, y, z, c: (x + 1 - 2 * c, y, z, c))


def along_y(value):
    return routed(value, lambda x, y, z, c: (x, y + 1 - 2 * c, z, c))


def along_z(value):
    return routed(value, lambda x, y, z, c: (x, y, z + 1 - 2 * c, c))


def across_z(value):
    return routed(value, lambda x, y, z, c: (x, y, z + 2, c))


def across_y(value):
    return routed(value, lambda x, y, z, c: (x, y + 2, z, c))


def mm(a, b):
    return jnp.dot(a, b, preferred_element_type=F32)


def complex_mm(ar, ai, br, bi):
    return mm(ar, br) - mm(ai, bi), mm(ar, bi) + mm(ai, br)


def rounded(pair):
    return pair[0].astype(BF16), pair[1].astype(BF16)


def slot_of(parent, x, p, c):
    dx = (parent // 4 - x + 4) % 4
    dp = ((parent // 2) % 2 + p) % 2
    dc = (parent % 2 + c) % 2
    near = dx == 3 - 2 * c
    side = jnp.where(near, jnp.where(dc == 0, 2, 6), jnp.where(dc == 0, 7, 3))
    side = side + 6 * dp
    base = jnp.where(dx == 0, dc + 4 * dp, 10 + dc + 4 * dp)
    return jnp.where((dx == 1) | (dx == 3), side, base)


def round_up(count):
    return jnp.floor((count + (PAD - 1)) * (1.0 / PAD)) * PAD


def iota(shape, axis):
    return lax.broadcasted_iota(jnp.int32, shape, axis)


def prepare_kernel(
    where_ref, parents_ref, rows_hbm, x1_ref, goes_ref, place_ref, table_ref, sel, rows_ref, sem
):
    copy = pltpu.make_async_copy(rows_hbm, rows_ref, sem)
    copy.start()
    x, p, c = where_ref[2], where_ref[3], where_ref[1]
    triangle = (iota((ROWS, ROWS), 0) < iota((ROWS, ROWS), 1)).astype(BF16)
    node = iota((NODES, ROWS), 0)
    match = jnp.concatenate(
        [
            (node == slot_of(parents_ref[0:1, :], x, p, c)).astype(F32),
            (node == slot_of(parents_ref[1:2, :], x, p, c)).astype(F32),
        ],
        axis=0,
    )
    before = mm(match.astype(BF16), triangle)
    total = round_up(jnp.sum(match, axis=1, keepdims=True))
    lower = (iota((NODES, NODES), 1) < iota((NODES, NODES), 0)).astype(BF16)
    upper = (iota((NODES, NODES), 0) < iota((NODES, NODES), 1)).astype(BF16)
    places, rows_of_table = [], []
    for way in range(2):
        own = match[way * NODES : (way + 1) * NODES]
        padded = jnp.broadcast_to(total[way * NODES : (way + 1) * NODES], (NODES, 128)).astype(BF16)
        start = mm(lower, padded)[:, :1]
        places.append(
            jnp.sum(own * (start + before[way * NODES : (way + 1) * NODES]), axis=0, keepdims=True)
        )
        count = lax.dot_general(
            jnp.ones((8, ROWS), BF16), own.astype(BF16), (((1,), (1,)), ((), ())), preferred_element_type=F32
        )
        rows_of_table += [mm(round_up(count).astype(BF16), upper), count]
    row = iota((8, NODES), 0)
    table = jnp.where(row == 0, rows_of_table[0], 0.0)
    for k in range(1, 4):
        table = jnp.where(row == k, rows_of_table[k], table)
    table_ref[...] = table.astype(jnp.int32)

    place1 = places[0].astype(jnp.int32)
    copy.wait()
    flat = rows_ref[...].reshape(ROWS, 2 * BOND)
    step = 256
    for block in range(SORTED // step):
        spot = pl.ds(block * step, step)
        one_hot = (iota((step, ROWS), 0) + block * step == place1).astype(BF16)
        sel[spot, :] = one_hot
        sorted_rows = mm(one_hot, flat).astype(BF16)
        x1_ref[0, spot, :] = sorted_rows[:, :BOND]
        x1_ref[1, spot, :] = sorted_rows[:, BOND:]
    x1_ref[:, pl.ds(SORTED, ROOM - SORTED), :] = jnp.zeros((2, ROOM - SORTED, BOND), BF16)

    high = jnp.floor(places[1] * (1.0 / 64.0))
    low = places[1] - 64.0 * high
    which = iota((8, ROWS), 0)
    parts = jnp.where(which == 0, high + 1.0, jnp.where(which == 1, low, 0.0)).astype(BF16)
    found = lax.dot_general(parts, sel[...], (((1,), (1,)), ((), ())), preferred_element_type=F32)
    goes_ref[...] = jnp.broadcast_to((found[0:1] - 1.0) * 64.0 + found[1:2], (8, SORTED)).astype(jnp.int32)
    place_ref[...] = jnp.broadcast_to(places[1], (8, ROWS))


def select_kernel(goes_ref, place_ref, to2_ref, back_ref):
    step = 256
    for block in range(SORTED // step):
        to2_ref[pl.ds(block * step, step), :] = (
            iota((step, SORTED), 0) + block * step == goes_ref[0:1, :]
        ).astype(BF16)
    column = jnp.transpose(jnp.broadcast_to(place_ref[0:1, :], (128, ROWS))).astype(jnp.int32)[:, :1]
    for block in range(ROWS // step):
        back_ref[pl.ds(block * step, step), :] = (
            iota((step, SORTED), 1) == column[block * step : (block + 1) * step]
        ).astype(BF16)


def window(x_ref, out_ref, slot, which, begin):
    spot = pl.ds(pl.multiple_of(begin, PAD), WINDOW)
    pair = x_ref[:, spot, :].reshape(2 * WINDOW, BOND)
    by_re, by_im = mm(pair, slot[which, 0]), mm(pair, slot[which, 1])
    out_ref[0, spot, :] = (by_re[:WINDOW] - by_im[WINDOW:]).astype(BF16)
    out_ref[1, spot, :] = (by_im[:WINDOW] + by_re[WINDOW:]).astype(BF16)


def level(x_ref, out_ref, table_ref, row, slots, which):
    out_ref[:, pl.ds(ROOM - TAIL, TAIL), :] = jnp.zeros((2, TAIL, BOND), BF16)
    for k, slot in enumerate(slots):
        @pl.when(table_ref[row + 1, k] > WINDOW)
        def _(k=k, slot=slot):
            window(x_ref, out_ref, slot, which, table_ref[row, k] + WINDOW)
    for k, slot in enumerate(slots):
        window(x_ref, out_ref, slot, which, table_ref[row, k])


def nodes_kernel(*refs):
    table_ref, x1_ref, to2_ref = refs[:3]
    slots = refs[3 : 3 + NODES]
    second, first, x2 = refs[3 + NODES :]
    level(x1_ref, first, table_ref, 0, slots, 0)
    x2[:, pl.ds(SORTED, ROOM - SORTED), :] = jnp.zeros((2, ROOM - SORTED, BOND), BF16)
    step = 256
    for block in range(SORTED // step):
        spot = pl.ds(block * step, step)
        for part in range(2):
            x2[part, spot, :] = mm(to2_ref[spot, :], first[part, pl.ds(0, SORTED), :]).astype(BF16)
    level(x2, second, table_ref, 2, slots, 1)


def stem_kernel(second, back_ref, ends_ref, far_ref, out_ref):
    left = rounded(complex_mm(ends_ref[0, 0], ends_ref[0, 1], far_ref[0], far_ref[1]))
    loop_re, loop_im = rounded(complex_mm(*left, ends_ref[1, 0], ends_ref[1, 1]))
    step = 256
    spread = iota((2 * step, 2 * step), 0)
    interleave = (iota((2 * step, 2 * step), 1) == spread // 2 + step * (spread % 2)).astype(BF16)
    for block in range(ROWS // step):
        spot = pl.ds(block * step, step)
        pair = jnp.concatenate(
            [mm(back_ref[spot, :], second[part, pl.ds(0, SORTED), :]).astype(BF16) for part in range(2)], axis=0
        )
        by_re, by_im = mm(pair, loop_re), mm(pair, loop_im)
        pair = jnp.concatenate([by_re[:step] - by_im[step:], by_im[:step] + by_re[step:]], axis=0)
        out_ref[spot] = mm(interleave, pair.astype(BF16)).astype(BF16).reshape(step, 2, BOND)


def pair_kernel(where_ref, own_ref, other_ref, p_ref, full):
    c = where_ref[1]
    for layer in range(2):
        for part in range(2):
            full[layer, part, pl.ds(pl.multiple_of(c * 128, 128), 128), :] = own_ref[layer, part]
            full[layer, part, pl.ds(pl.multiple_of((1 - c) * 128, 128), 128), :] = other_ref[layer, part]
    re, im = complex_mm(full[0, 0], full[0, 1], full[1, 0], full[1, 1])
    p_ref[0] = re.astype(BF16)
    p_ref[1] = im.astype(BF16)


def gather_ring(where_ref, refs, held):
    z, c = where_ref[0], where_ref[1]
    spots = (z, (z + 3 + 2 * c) % 4, (z + 1 + 2 - 2 * c + 2) % 4, (z + 2) % 4)
    for spot, ref in zip(spots, refs):
        held[spot] = ref[...]


def ring_kernel(where_ref, a_ref, b_ref, c_ref, d_ref, t_ref, held):
    gather_ring(where_ref, (a_ref, b_ref, c_ref, d_ref), held)
    re, im = held[0, 0], held[0, 1]
    for spot in (1, 2, 3):
        re, im = rounded(complex_mm(re, im, held[spot, 0], held[spot, 1]))
    t_ref[0] = re
    t_ref[1] = im


def ends_kernel(where_ref, a_ref, b_ref, c_ref, d_ref, ends_ref, held):
    gather_ring(where_ref, (a_ref, b_ref, c_ref, d_ref), held)
    z = where_ref[0]
    ends_ref[0] = held[z]
    ends_ref[1, 0] = (iota((BOND, BOND), 0) == iota((BOND, BOND), 1)).astype(BF16)
    ends_ref[1, 1] = jnp.zeros((BOND, BOND), BF16)
    for i in range(1, 4):
        end = jnp.where(z + i < 4, 0, 1)
        spot = (z + i) % 4
        re, im = rounded(complex_mm(ends_ref[end, 0], ends_ref[end, 1], held[spot, 0], held[spot, 1]))
        ends_ref[end, 0] = re
        ends_ref[end, 1] = im


def vmem():
    return pl.BlockSpec(memory_space=pltpu.VMEM)


def smem():
    return pl.BlockSpec(memory_space=pltpu.SMEM)


def call(kernel, out, ins, scratch, flops, moved, room=20):
    return pl.pallas_call(
        kernel,
        out_shape=out,
        in_specs=ins,
        out_specs=jax.tree.map(lambda _: vmem(), out),
        scratch_shapes=scratch,
        cost_estimate=pl.CostEstimate(flops=1024, bytes_accessed=1024, transcendentals=0),
        compiler_params=pltpu.CompilerParams(vmem_limit_bytes=room * 2**20),
    )


def shared(value):
    with jax.named_scope("shared"):
        return swap(value)


def after(value, *others):
    return lax.optimization_barrier((value, *others))[0]


def body(branch_rows, first_parent, second_parent, node_first, node_second, stem_tensors):
    stem, leaf, core = (lax.axis_index(name) for name in AXES)
    where = jnp.stack([stem % 4, core, leaf // 2, leaf % 2]).astype(jnp.int32)
    matrix = jax.ShapeDtypeStruct((2, BOND, BOND), BF16)

    own = lax.optimization_barrier(jnp.concatenate([node_first, node_second], axis=0))
    with jax.named_scope("side"):
        side = along_x(own)
    with jax.named_scope("sibling"):
        sibling = swap(own)
    stem_own = stem_tensors[0]
    with jax.named_scope("stem_other"):
        stem_other = swap(stem_own)
    own_later, sibling_later = lax.optimization_barrier((own, sibling))[:2]
    with jax.named_scope("side_far"):
        side_far = along_x(sibling_later)
    with jax.named_scope("turned"):
        turned = along_y(own_later)
    product = call(pair_kernel, matrix, [smem(), vmem(), vmem()],
                   [pltpu.VMEM((2, 2, BOND, BOND), BF16)], 2**28, 2**20)(after(where, sibling), stem_own, stem_other)
    with jax.named_scope("side_turned"):
        side_turned = along_y(after(side, product, turned))
    with jax.named_scope("across"):
        across = along_x(after(side, product, turned))
    with jax.named_scope("near"):
        near = along_z(product)
    with jax.named_scope("opposite"):
        opposite = across_z(product)
    with jax.named_scope("near_other"):
        near_other = swap(near)
    with jax.named_scope("side_far_turned"):
        side_far_turned = along_y(after(side_far, product))
    with jax.named_scope("across_turned"):
        across_turned = along_x(side_turned)
    ring = (product, near, near_other, opposite)
    total = call(ring_kernel, matrix, [smem()] + [vmem()] * 4,
                 [pltpu.VMEM((4, 2, BOND, BOND), BF16)], 2**29, 2**20)(where, *ring)
    with jax.named_scope("far"):
        far = across_y(total)
    hbm = pl.BlockSpec(memory_space=pltpu.HBM)
    parents = jnp.concatenate([first_parent.reshape(1, ROWS), second_parent.reshape(1, ROWS)], axis=0)
    x1, goes, place, table = call(
        prepare_kernel,
        (
            jax.ShapeDtypeStruct((2, ROOM, BOND), BF16),
            jax.ShapeDtypeStruct((8, SORTED), jnp.int32),
            jax.ShapeDtypeStruct((8, ROWS), F32),
            jax.ShapeDtypeStruct((8, NODES), jnp.int32),
        ),
        [smem(), vmem(), hbm],
        [
            pltpu.VMEM((SORTED, ROWS), BF16),
            pltpu.VMEM((ROWS, 2, BOND), BF16),
            pltpu.SemaphoreType.DMA,
        ],
        2**31, 2**22,
    )(after(where, total, across), parents, branch_rows)
    to2, back = call(
        select_kernel,
        (jax.ShapeDtypeStruct((SORTED, SORTED), BF16), jax.ShapeDtypeStruct((ROWS, SORTED), BF16)),
        [vmem(), vmem()], [], 2**30, 2**22,
    )(after(goes, side_turned), place)
    ends = call(ends_kernel, jax.ShapeDtypeStruct((2, 2, BOND, BOND), BF16), [smem()] + [vmem()] * 4,
                [pltpu.VMEM((4, 2, BOND, BOND), BF16)], 2**29, 2**20)(after(where, table), *ring)

    side_shared = shared(after(side, table))
    turned_shared = shared(after(turned, table))
    side_far_shared = shared(after(side_far, table))
    side_turned_shared = shared(after(side_turned, table))
    across_shared = shared(after(across, table))
    side_far_turned_shared = shared(after(side_far_turned, table))
    across_turned_shared = shared(after(across_turned, to2, ends))
    pairs = (
        (own, sibling), (side, side_shared), (turned, turned_shared), (side_far, side_far_shared),
        (side_turned, side_turned_shared), (across, across_shared),
        (side_far_turned, side_far_turned_shared), (across_turned, across_turned_shared),
    )
    slots = [value for pair in pairs for value in pair]

    second = call(
        nodes_kernel,
        jax.ShapeDtypeStruct((2, ROOM, BOND), BF16),
        [smem()] + [vmem()] * (2 + NODES),
        [pltpu.VMEM((2, ROOM, BOND), BF16)] * 2,
        2**33, 2**24,
    )(table, x1, to2, *slots)
    return call(
        stem_kernel, jax.ShapeDtypeStruct((ROWS, 2, BOND), BF16), [vmem()] * 4, [], 2**32, 2**23
    )(second, back, ends, after(far, second))


def solution(mesh):
    return jax.shard_map(
        body,
        mesh=mesh,
        in_specs=(
            P(AXES, None, None),
            P(AXES, None),
            P(AXES, None),
            P(("leaf", "slab"), None, None, None),
            P(("leaf", "slab"), None, None, None),
            P("stem", None, None, "slab", None),
        ),
        out_specs=P(AXES, None, None),
        check_vma=False,
    )
```

```python
import jax
import jax.numpy as jnp
from jax import lax
from jax.experimental import pallas as pl
from jax.experimental.pallas import tpu as pltpu
from jax.sharding import PartitionSpec as P

AXES = ("stem", "leaf", "slab")
ROWS = 1024
BOND = 256
NODES = 16
PAD = 16
SORTED = 1280
CAP = 160
ROOM = SORTED + CAP
TAIL = ROOM - 928
F32 = jnp.float32
BF16 = jnp.bfloat16


def device_index(x, y, z, c):
    return (((y // 2) * 4 + z) * 8 + (x * 2 + y % 2)) * 2 + c


def routed(value, move):
    pairs = []
    for x in range(4):
        for y in range(4):
            for z in range(4):
                for c in range(2):
                    tx, ty, tz, tc = move(x, y, z, c)
                    pairs.append((device_index(x, y, z, c), device_index(tx % 4, ty % 4, tz % 4, tc)))
    return lax.ppermute(value, AXES, pairs)


def swap(value):
    return routed(value, lambda x, y, z, c: (x, y, z, 1 - c))


def along_x(value):
    return routed(value, lambda x, y, z, c: (x + 1 - 2 * c, y, z, c))


def along_y(value):
    return routed(value, lambda x, y, z, c: (x, y + 1 - 2 * c, z, c))


def along_z(value):
    return routed(value, lambda x, y, z, c: (x, y, z + 1 - 2 * c, c))


def across_z(value):
    return routed(value, lambda x, y, z, c: (x, y, z + 2, c))


def across_y(value):
    return routed(value, lambda x, y, z, c: (x, y + 2, z, c))


def mm(a, b):
    return jnp.dot(a, b, preferred_element_type=F32)


def complex_mm(ar, ai, br, bi):
    return mm(ar, br) - mm(ai, bi), mm(ar, bi) + mm(ai, br)


def rounded(pair):
    return pair[0].astype(BF16), pair[1].astype(BF16)


def slot_of(parent, x, p, c):
    dx = (parent // 4 - x + 4) % 4
    dp = ((parent // 2) % 2 + p) % 2
    dc = (parent % 2 + c) % 2
    near = dx == 3 - 2 * c
    side = jnp.where(near, jnp.where(dc == 0, 2, 6), jnp.where(dc == 0, 7, 3))
    side = side + 6 * dp
    base = jnp.where(dx == 0, dc + 4 * dp, 10 + dc + 4 * dp)
    return jnp.where((dx == 1) | (dx == 3), side, base)


def round_up(count):
    return jnp.floor((count + (PAD - 1)) * (1.0 / PAD)) * PAD


def iota(shape, axis):
    return lax.broadcasted_iota(jnp.int32, shape, axis)


def prepare_kernel(
    where_ref, parents_ref, rows_hbm, x1_ref, goes_ref, place_ref, table_ref, sel, rows_ref, sem
):
    copy = pltpu.make_async_copy(rows_hbm, rows_ref, sem)
    copy.start()
    x, p, c = where_ref[2], where_ref[3], where_ref[1]
    triangle = (iota((ROWS, ROWS), 0) < iota((ROWS, ROWS), 1)).astype(BF16)
    node = iota((NODES, ROWS), 0)
    match = jnp.concatenate(
        [
            (node == slot_of(parents_ref[0:1, :], x, p, c)).astype(F32),
            (node == slot_of(parents_ref[1:2, :], x, p, c)).astype(F32),
        ],
        axis=0,
    )
    before = mm(match.astype(BF16), triangle)
    total = round_up(jnp.sum(match, axis=1, keepdims=True))
    lower = (iota((NODES, NODES), 1) < iota((NODES, NODES), 0)).astype(BF16)
    upper = (iota((NODES, NODES), 0) < iota((NODES, NODES), 1)).astype(BF16)
    places, rows_of_table = [], []
    for way in range(2):
        own = match[way * NODES : (way + 1) * NODES]
        padded = jnp.broadcast_to(total[way * NODES : (way + 1) * NODES], (NODES, 128)).astype(BF16)
        start = mm(lower, padded)[:, :1]
        places.append(
            jnp.sum(own * (start + before[way * NODES : (way + 1) * NODES]), axis=0, keepdims=True)
        )
        count = lax.dot_general(
            jnp.ones((8, ROWS), BF16), own.astype(BF16), (((1,), (1,)), ((), ())), preferred_element_type=F32
        )
        rows_of_table += [mm(round_up(count).astype(BF16), upper), count]
    row = iota((8, NODES), 0)
    table = jnp.where(row == 0, rows_of_table[0], 0.0)
    for k in range(1, 4):
        table = jnp.where(row == k, rows_of_table[k], table)
    table_ref[...] = table.astype(jnp.int32)

    place1 = places[0].astype(jnp.int32)
    copy.wait()
    flat = rows_ref[...].reshape(ROWS, 2 * BOND)
    step = 256
    for block in range(SORTED // step):
        spot = pl.ds(block * step, step)
        one_hot = (iota((step, ROWS), 0) + block * step == place1).astype(BF16)
        sel[spot, :] = one_hot
        sorted_rows = mm(one_hot, flat).astype(BF16)
        x1_ref[0, spot, :] = sorted_rows[:, :BOND]
        x1_ref[1, spot, :] = sorted_rows[:, BOND:]
    x1_ref[:, pl.ds(SORTED, ROOM - SORTED), :] = jnp.zeros((2, ROOM - SORTED, BOND), BF16)

    high = jnp.floor(places[1] * (1.0 / 64.0))
    low = places[1] - 64.0 * high
    which = iota((8, ROWS), 0)
    parts = jnp.where(which == 0, high + 1.0, jnp.where(which == 1, low, 0.0)).astype(BF16)
    found = lax.dot_general(parts, sel[...], (((1,), (1,)), ((), ())), preferred_element_type=F32)
    goes_ref[...] = jnp.broadcast_to((found[0:1] - 1.0) * 64.0 + found[1:2], (8, SORTED)).astype(jnp.int32)
    place_ref[...] = jnp.broadcast_to(places[1], (8, ROWS))


def select_kernel(goes_ref, place_ref, to2_ref, back_ref):
    step = 256
    for block in range(SORTED // step):
        to2_ref[pl.ds(block * step, step), :] = (
            iota((step, SORTED), 0) + block * step == goes_ref[0:1, :]
        ).astype(BF16)
    column = jnp.transpose(jnp.broadcast_to(place_ref[0:1, :], (128, ROWS))).astype(jnp.int32)[:, :1]
    for block in range(ROWS // step):
        back_ref[pl.ds(block * step, step), :] = (
            iota((step, SORTED), 1) == column[block * step : (block + 1) * step]
        ).astype(BF16)


def window(x_ref, out_ref, slot, which, begin):
    spot = pl.ds(pl.multiple_of(begin, PAD), CAP)
    pair = x_ref[:, spot, :].reshape(2 * CAP, BOND)
    by_re, by_im = mm(pair, slot[which, 0]), mm(pair, slot[which, 1])
    out_ref[0, spot, :] = (by_re[:CAP] - by_im[CAP:]).astype(BF16)
    out_ref[1, spot, :] = (by_im[:CAP] + by_re[CAP:]).astype(BF16)


def level(x_ref, out_ref, table_ref, row, slots, which):
    out_ref[:, pl.ds(ROOM - TAIL, TAIL), :] = jnp.zeros((2, TAIL, BOND), BF16)
    for k, slot in enumerate(slots):
        window(x_ref, out_ref, slot, which, table_ref[row, k])


def nodes_kernel(*refs):
    table_ref, x1_ref, to2_ref = refs[:3]
    slots = refs[3 : 3 + NODES]
    second, first, x2 = refs[3 + NODES :]
    level(x1_ref, first, table_ref, 0, slots, 0)
    x2[:, pl.ds(SORTED, ROOM - SORTED), :] = jnp.zeros((2, ROOM - SORTED, BOND), BF16)
    step = 256
    for block in range(SORTED // step):
        spot = pl.ds(block * step, step)
        for part in range(2):
            x2[part, spot, :] = mm(to2_ref[spot, :], first[part, pl.ds(0, SORTED), :]).astype(BF16)
    level(x2, second, table_ref, 2, slots, 1)


def stem_kernel(second, back_ref, ends_ref, far_ref, out_ref):
    left = rounded(complex_mm(ends_ref[0, 0], ends_ref[0, 1], far_ref[0], far_ref[1]))
    loop_re, loop_im = rounded(complex_mm(*left, ends_ref[1, 0], ends_ref[1, 1]))
    step = 256
    spread = iota((2 * step, 2 * step), 0)
    interleave = (iota((2 * step, 2 * step), 1) == spread // 2 + step * (spread % 2)).astype(BF16)
    for block in range(ROWS // step):
        spot = pl.ds(block * step, step)
        pair = jnp.concatenate(
            [mm(back_ref[spot, :], second[part, pl.ds(0, SORTED), :]).astype(BF16) for part in range(2)], axis=0
        )
        by_re, by_im = mm(pair, loop_re), mm(pair, loop_im)
        pair = jnp.concatenate([by_re[:step] - by_im[step:], by_im[:step] + by_re[step:]], axis=0)
        out_ref[spot] = mm(interleave, pair.astype(BF16)).astype(BF16).reshape(step, 2, BOND)


def pair_kernel(where_ref, own_ref, other_ref, p_ref, full):
    c = where_ref[1]
    for layer in range(2):
        for part in range(2):
            full[layer, part, pl.ds(pl.multiple_of(c * 128, 128), 128), :] = own_ref[layer, part]
            full[layer, part, pl.ds(pl.multiple_of((1 - c) * 128, 128), 128), :] = other_ref[layer, part]
    re, im = complex_mm(full[0, 0], full[0, 1], full[1, 0], full[1, 1])
    p_ref[0] = re.astype(BF16)
    p_ref[1] = im.astype(BF16)


def gather_ring(where_ref, refs, held):
    z, c = where_ref[0], where_ref[1]
    spots = (z, (z + 3 + 2 * c) % 4, (z + 1 + 2 - 2 * c + 2) % 4, (z + 2) % 4)
    for spot, ref in zip(spots, refs):
        held[spot] = ref[...]


def ring_kernel(where_ref, a_ref, b_ref, c_ref, d_ref, t_ref, held):
    gather_ring(where_ref, (a_ref, b_ref, c_ref, d_ref), held)
    re, im = held[0, 0], held[0, 1]
    for spot in (1, 2, 3):
        re, im = rounded(complex_mm(re, im, held[spot, 0], held[spot, 1]))
    t_ref[0] = re
    t_ref[1] = im


def ends_kernel(where_ref, a_ref, b_ref, c_ref, d_ref, ends_ref, held):
    gather_ring(where_ref, (a_ref, b_ref, c_ref, d_ref), held)
    z = where_ref[0]
    ends_ref[0] = held[z]
    ends_ref[1, 0] = (iota((BOND, BOND), 0) == iota((BOND, BOND), 1)).astype(BF16)
    ends_ref[1, 1] = jnp.zeros((BOND, BOND), BF16)
    for i in range(1, 4):
        end = jnp.where(z + i < 4, 0, 1)
        spot = (z + i) % 4
        re, im = rounded(complex_mm(ends_ref[end, 0], ends_ref[end, 1], held[spot, 0], held[spot, 1]))
        ends_ref[end, 0] = re
        ends_ref[end, 1] = im


def vmem():
    return pl.BlockSpec(memory_space=pltpu.VMEM)


def smem():
    return pl.BlockSpec(memory_space=pltpu.SMEM)


def call(kernel, out, ins, scratch, flops, moved, room=20):
    return pl.pallas_call(
        kernel,
        out_shape=out,
        in_specs=ins,
        out_specs=jax.tree.map(lambda _: vmem(), out),
        scratch_shapes=scratch,
        cost_estimate=pl.CostEstimate(flops=1024, bytes_accessed=1024, transcendentals=0),
        compiler_params=pltpu.CompilerParams(vmem_limit_bytes=room * 2**20),
    )


def shared(value):
    with jax.named_scope("shared"):
        return swap(value)


def after(value, *others):
    return lax.optimization_barrier((value, *others))[0]


def body(branch_rows, first_parent, second_parent, node_first, node_second, stem_tensors):
    stem, leaf, core = (lax.axis_index(name) for name in AXES)
    where = jnp.stack([stem % 4, core, leaf // 2, leaf % 2]).astype(jnp.int32)
    matrix = jax.ShapeDtypeStruct((2, BOND, BOND), BF16)

    own = lax.optimization_barrier(jnp.concatenate([node_first, node_second], axis=0))
    with jax.named_scope("side"):
        side = along_x(own)
    with jax.named_scope("sibling"):
        sibling = swap(own)
    stem_own = stem_tensors[0]
    with jax.named_scope("stem_other"):
        stem_other = swap(stem_own)
    own_later, sibling_later = lax.optimization_barrier((own, sibling))[:2]
    with jax.named_scope("side_far"):
        side_far = along_x(sibling_later)
    with jax.named_scope("turned"):
        turned = along_y(own_later)
    product = call(pair_kernel, matrix, [smem(), vmem(), vmem()],
                   [pltpu.VMEM((2, 2, BOND, BOND), BF16)], 2**28, 2**20)(after(where, sibling), stem_own, stem_other)
    with jax.named_scope("side_turned"):
        side_turned = along_y(after(side, product, turned))
    with jax.named_scope("across"):
        across = along_x(after(side, product, turned))
    with jax.named_scope("near"):
        near = along_z(product)
    with jax.named_scope("opposite"):
        opposite = across_z(product)
    with jax.named_scope("near_other"):
        near_other = swap(near)
    with jax.named_scope("side_far_turned"):
        side_far_turned = along_y(after(side_far, product))
    with jax.named_scope("across_turned"):
        across_turned = along_x(side_turned)
    ring = (product, near, near_other, opposite)
    total = call(ring_kernel, matrix, [smem()] + [vmem()] * 4,
                 [pltpu.VMEM((4, 2, BOND, BOND), BF16)], 2**29, 2**20)(where, *ring)
    with jax.named_scope("far"):
        far = across_y(total)
    hbm = pl.BlockSpec(memory_space=pltpu.HBM)
    parents = jnp.concatenate([first_parent.reshape(1, ROWS), second_parent.reshape(1, ROWS)], axis=0)
    x1, goes, place, table = call(
        prepare_kernel,
        (
            jax.ShapeDtypeStruct((2, ROOM, BOND), BF16),
            jax.ShapeDtypeStruct((8, SORTED), jnp.int32),
            jax.ShapeDtypeStruct((8, ROWS), F32),
            jax.ShapeDtypeStruct((8, NODES), jnp.int32),
        ),
        [smem(), vmem(), hbm],
        [
            pltpu.VMEM((SORTED, ROWS), BF16),
            pltpu.VMEM((ROWS, 2, BOND), BF16),
            pltpu.SemaphoreType.DMA,
        ],
        2**31, 2**22,
    )(after(where, total, across), parents, branch_rows)
    to2, back = call(
        select_kernel,
        (jax.ShapeDtypeStruct((SORTED, SORTED), BF16), jax.ShapeDtypeStruct((ROWS, SORTED), BF16)),
        [vmem(), vmem()], [], 2**30, 2**22,
    )(after(goes, side_turned), place)
    ends = call(ends_kernel, jax.ShapeDtypeStruct((2, 2, BOND, BOND), BF16), [smem()] + [vmem()] * 4,
                [pltpu.VMEM((4, 2, BOND, BOND), BF16)], 2**29, 2**20)(after(where, table), *ring)

    side_shared = shared(after(side, table))
    turned_shared = shared(after(turned, table))
    side_far_shared = shared(after(side_far, table))
    side_turned_shared = shared(after(side_turned, table))
    across_shared = shared(after(across, table))
    side_far_turned_shared = shared(after(side_far_turned, table))
    across_turned_shared = shared(after(across_turned, to2, ends))
    pairs = (
        (own, sibling), (side, side_shared), (turned, turned_shared), (side_far, side_far_shared),
        (side_turned, side_turned_shared), (across, across_shared),
        (side_far_turned, side_far_turned_shared), (across_turned, across_turned_shared),
    )
    slots = [value for pair in pairs for value in pair]

    second = call(
        nodes_kernel,
        jax.ShapeDtypeStruct((2, ROOM, BOND), BF16),
        [smem()] + [vmem()] * (2 + NODES),
        [pltpu.VMEM((2, ROOM, BOND), BF16)] * 2,
        2**33, 2**24,
    )(table, x1, to2, *slots)
    return call(
        stem_kernel, jax.ShapeDtypeStruct((ROWS, 2, BOND), BF16), [vmem()] * 4, [], 2**32, 2**23
    )(second, back, ends, after(far, second))


def solution(mesh):
    return jax.shard_map(
        body,
        mesh=mesh,
        in_specs=(
            P(AXES, None, None),
            P(AXES, None),
            P(AXES, None),
            P(("leaf", "slab"), None, None, None),
            P(("leaf", "slab"), None, None, None),
            P("stem", None, None, "slab", None),
        ),
        out_specs=P(AXES, None, None),
        check_vma=False,
    )
```

```python
import jax
import jax.numpy as jnp
from jax import lax
from jax.experimental import pallas as pl
from jax.experimental.pallas import tpu as pltpu
from jax.sharding import PartitionSpec as P

AXES = ("stem", "leaf", "slab")
ROWS = 1024
BOND = 256
NODES = 16
PAD = 16
SORTED = 1280
WINDOW = 80
ROOM = SORTED + 2 * WINDOW
TAIL = ROOM - 928
F32 = jnp.float32
BF16 = jnp.bfloat16


def device_index(x, y, z, c):
    return (((y // 2) * 4 + z) * 8 + (x * 2 + y % 2)) * 2 + c


def routed(value, move):
    pairs = []
    for x in range(4):
        for y in range(4):
            for z in range(4):
                for c in range(2):
                    tx, ty, tz, tc = move(x, y, z, c)
                    pairs.append((device_index(x, y, z, c), device_index(tx % 4, ty % 4, tz % 4, tc)))
    return lax.ppermute(value, AXES, pairs)


def swap(value):
    return routed(value, lambda x, y, z, c: (x, y, z, 1 - c))


def along_x(value):
    return routed(value, lambda x, y, z, c: (x + 1 - 2 * c, y, z, c))


def along_y(value):
    return routed(value, lambda x, y, z, c: (x, y + 1 - 2 * c, z, c))


def along_z(value):
    return routed(value, lambda x, y, z, c: (x, y, z + 1 - 2 * c, c))


def across_z(value):
    return routed(value, lambda x, y, z, c: (x, y, z + 2, c))


def across_y(value):
    return routed(value, lambda x, y, z, c: (x, y + 2, z, c))


def mm(a, b):
    return jnp.dot(a, b, preferred_element_type=F32)


def complex_mm(ar, ai, br, bi):
    return mm(ar, br) - mm(ai, bi), mm(ar, bi) + mm(ai, br)


def rounded(pair):
    return pair[0].astype(BF16), pair[1].astype(BF16)


def slot_of(parent, x, p, c):
    dx = (parent // 4 - x + 4) % 4
    dp = ((parent // 2) % 2 + p) % 2
    dc = (parent % 2 + c) % 2
    near = dx == 3 - 2 * c
    side = jnp.where(near, jnp.where(dc == 0, 2, 6), jnp.where(dc == 0, 7, 3))
    side = side + 6 * dp
    base = jnp.where(dx == 0, dc + 4 * dp, 10 + dc + 4 * dp)
    return jnp.where((dx == 1) | (dx == 3), side, base)


def round_up(count):
    return jnp.floor((count + (PAD - 1)) * (1.0 / PAD)) * PAD


def iota(shape, axis):
    return lax.broadcasted_iota(jnp.int32, shape, axis)


def prepare_kernel(
    where_ref, parents_ref, rows_hbm, x1_ref, goes_ref, place_ref, table_ref, sel, rows_ref, sem
):
    copy = pltpu.make_async_copy(rows_hbm, rows_ref, sem)
    copy.start()
    x, p, c = where_ref[2], where_ref[3], where_ref[1]
    step = 256
    triangle = (iota((step, step), 0) < iota((step, step), 1)).astype(BF16)
    node = iota((NODES, ROWS), 0)
    match = jnp.concatenate(
        [
            (node == slot_of(parents_ref[0:1, :], x, p, c)).astype(F32),
            (node == slot_of(parents_ref[1:2, :], x, p, c)).astype(F32),
        ],
        axis=0,
    )
    before, passed = [], jnp.zeros((2 * NODES, 1), F32)
    for block in range(ROWS // step):
        piece = match[:, block * step : (block + 1) * step]
        before.append(mm(piece.astype(BF16), triangle) + passed)
        passed = passed + jnp.sum(piece, axis=1, keepdims=True)
    before = jnp.concatenate(before, axis=1)
    total = round_up(passed)
    lower = (iota((NODES, NODES), 1) < iota((NODES, NODES), 0)).astype(BF16)
    upper = (iota((NODES, NODES), 0) < iota((NODES, NODES), 1)).astype(BF16)
    places, rows_of_table = [], []
    for way in range(2):
        own = match[way * NODES : (way + 1) * NODES]
        padded = jnp.broadcast_to(total[way * NODES : (way + 1) * NODES], (NODES, 128)).astype(BF16)
        start = mm(lower, padded)[:, :1]
        places.append(
            jnp.sum(own * (start + before[way * NODES : (way + 1) * NODES]), axis=0, keepdims=True)
        )
        count = lax.dot_general(
            jnp.ones((8, ROWS), BF16), own.astype(BF16), (((1,), (1,)), ((), ())), preferred_element_type=F32
        )
        rows_of_table += [mm(round_up(count).astype(BF16), upper), count]
    row = iota((8, NODES), 0)
    table = jnp.where(row == 0, rows_of_table[0], 0.0)
    for k in range(1, 4):
        table = jnp.where(row == k, rows_of_table[k], table)
    table_ref[...] = table.astype(jnp.int32)

    place1 = places[0].astype(jnp.int32)
    copy.wait()
    flat = rows_ref[...].reshape(ROWS, 2 * BOND)
    step = 256
    for block in range(SORTED // step):
        spot = pl.ds(block * step, step)
        one_hot = (iota((step, ROWS), 0) + block * step == place1).astype(BF16)
        sel[spot, :] = one_hot
        sorted_rows = mm(one_hot, flat).astype(BF16)
        x1_ref[0, spot, :] = sorted_rows[:, :BOND]
        x1_ref[1, spot, :] = sorted_rows[:, BOND:]
    x1_ref[:, pl.ds(SORTED, ROOM - SORTED), :] = jnp.zeros((2, ROOM - SORTED, BOND), BF16)

    high = jnp.floor(places[1] * (1.0 / 64.0))
    low = places[1] - 64.0 * high
    which = iota((8, ROWS), 0)
    parts = jnp.where(which == 0, high + 1.0, jnp.where(which == 1, low, 0.0)).astype(BF16)
    found = lax.dot_general(parts, sel[...], (((1,), (1,)), ((), ())), preferred_element_type=F32)
    goes_ref[...] = jnp.broadcast_to((found[0:1] - 1.0) * 64.0 + found[1:2], (8, SORTED)).astype(jnp.int32)
    place_ref[...] = jnp.broadcast_to(places[1], (8, ROWS))


def select_kernel(goes_ref, place_ref, to2_ref, back_ref):
    step = 256
    for block in range(SORTED // step):
        to2_ref[pl.ds(block * step, step), :] = (
            iota((step, SORTED), 0) + block * step == goes_ref[0:1, :]
        ).astype(BF16)
    column = jnp.transpose(jnp.broadcast_to(place_ref[0:1, :], (128, ROWS))).astype(jnp.int32)[:, :1]
    for block in range(ROWS // step):
        back_ref[pl.ds(block * step, step), :] = (
            iota((step, SORTED), 1) == column[block * step : (block + 1) * step]
        ).astype(BF16)


def window(x_ref, out_ref, slot, which, begin):
    spot = pl.ds(pl.multiple_of(begin, PAD), WINDOW)
    pair = x_ref[:, spot, :].reshape(2 * WINDOW, BOND)
    by_re, by_im = mm(pair, slot[which, 0]), mm(pair, slot[which, 1])
    out_ref[0, spot, :] = (by_re[:WINDOW] - by_im[WINDOW:]).astype(BF16)
    out_ref[1, spot, :] = (by_im[:WINDOW] + by_re[WINDOW:]).astype(BF16)


def level(x_ref, out_ref, table_ref, row, slots, which):
    out_ref[:, pl.ds(ROOM - TAIL, TAIL), :] = jnp.zeros((2, TAIL, BOND), BF16)
    for k, slot in enumerate(slots):
        @pl.when(table_ref[row + 1, k] > WINDOW)
        def _(k=k, slot=slot):
            window(x_ref, out_ref, slot, which, table_ref[row, k] + WINDOW)
    for k, slot in enumerate(slots):
        window(x_ref, out_ref, slot, which, table_ref[row, k])


def nodes_kernel(*refs):
    table_ref, x1_ref, to2_ref = refs[:3]
    slots = refs[3 : 3 + NODES]
    second, first, x2 = refs[3 + NODES :]
    level(x1_ref, first, table_ref, 0, slots, 0)
    x2[:, pl.ds(SORTED, ROOM - SORTED), :] = jnp.zeros((2, ROOM - SORTED, BOND), BF16)
    step = 256
    for block in range(SORTED // step):
        spot = pl.ds(block * step, step)
        for part in range(2):
            x2[part, spot, :] = mm(to2_ref[spot, :], first[part, pl.ds(0, SORTED), :]).astype(BF16)
    level(x2, second, table_ref, 2, slots, 1)


def stem_kernel(second, back_ref, ends_ref, far_ref, out_ref):
    left = rounded(complex_mm(ends_ref[0, 0], ends_ref[0, 1], far_ref[0], far_ref[1]))
    loop_re, loop_im = rounded(complex_mm(*left, ends_ref[1, 0], ends_ref[1, 1]))
    step = 256
    spread = iota((2 * step, 2 * step), 0)
    interleave = (iota((2 * step, 2 * step), 1) == spread // 2 + step * (spread % 2)).astype(BF16)
    for block in range(ROWS // step):
        spot = pl.ds(block * step, step)
        pair = jnp.concatenate(
            [mm(back_ref[spot, :], second[part, pl.ds(0, SORTED), :]).astype(BF16) for part in range(2)], axis=0
        )
        by_re, by_im = mm(pair, loop_re), mm(pair, loop_im)
        pair = jnp.concatenate([by_re[:step] - by_im[step:], by_im[:step] + by_re[step:]], axis=0)
        out_ref[spot] = mm(interleave, pair.astype(BF16)).astype(BF16).reshape(step, 2, BOND)


def pair_kernel(where_ref, own_ref, other_ref, p_ref, full):
    c = where_ref[1]
    for layer in range(2):
        for part in range(2):
            full[layer, part, pl.ds(pl.multiple_of(c * 128, 128), 128), :] = own_ref[layer, part]
            full[layer, part, pl.ds(pl.multiple_of((1 - c) * 128, 128), 128), :] = other_ref[layer, part]
    re, im = complex_mm(full[0, 0], full[0, 1], full[1, 0], full[1, 1])
    p_ref[0] = re.astype(BF16)
    p_ref[1] = im.astype(BF16)


def gather_ring(where_ref, refs, held):
    z, c = where_ref[0], where_ref[1]
    spots = (z, (z + 3 + 2 * c) % 4, (z + 1 + 2 - 2 * c + 2) % 4, (z + 2) % 4)
    for spot, ref in zip(spots, refs):
        held[spot] = ref[...]


def ring_kernel(where_ref, a_ref, b_ref, c_ref, d_ref, t_ref, held):
    gather_ring(where_ref, (a_ref, b_ref, c_ref, d_ref), held)
    re, im = held[0, 0], held[0, 1]
    for spot in (1, 2, 3):
        re, im = rounded(complex_mm(re, im, held[spot, 0], held[spot, 1]))
    t_ref[0] = re
    t_ref[1] = im


def ends_kernel(where_ref, a_ref, b_ref, c_ref, d_ref, ends_ref, held):
    gather_ring(where_ref, (a_ref, b_ref, c_ref, d_ref), held)
    z = where_ref[0]
    ends_ref[0] = held[z]
    ends_ref[1, 0] = (iota((BOND, BOND), 0) == iota((BOND, BOND), 1)).astype(BF16)
    ends_ref[1, 1] = jnp.zeros((BOND, BOND), BF16)
    for i in range(1, 4):
        end = jnp.where(z + i < 4, 0, 1)
        spot = (z + i) % 4
        re, im = rounded(complex_mm(ends_ref[end, 0], ends_ref[end, 1], held[spot, 0], held[spot, 1]))
        ends_ref[end, 0] = re
        ends_ref[end, 1] = im


def vmem():
    return pl.BlockSpec(memory_space=pltpu.VMEM)


def smem():
    return pl.BlockSpec(memory_space=pltpu.SMEM)


def call(kernel, out, ins, scratch, flops, moved, room=20):
    return pl.pallas_call(
        kernel,
        out_shape=out,
        in_specs=ins,
        out_specs=jax.tree.map(lambda _: vmem(), out),
        scratch_shapes=scratch,
        cost_estimate=pl.CostEstimate(flops=1024, bytes_accessed=1024, transcendentals=0),
        compiler_params=pltpu.CompilerParams(vmem_limit_bytes=room * 2**20),
    )


def shared(value):
    with jax.named_scope("shared"):
        return swap(value)


def after(value, *others):
    return lax.optimization_barrier((value, *others))[0]


def body(branch_rows, first_parent, second_parent, node_first, node_second, stem_tensors):
    stem, leaf, core = (lax.axis_index(name) for name in AXES)
    where = jnp.stack([stem % 4, core, leaf // 2, leaf % 2]).astype(jnp.int32)
    matrix = jax.ShapeDtypeStruct((2, BOND, BOND), BF16)

    own = lax.optimization_barrier(jnp.concatenate([node_first, node_second], axis=0))
    with jax.named_scope("side"):
        side = along_x(own)
    with jax.named_scope("sibling"):
        sibling = swap(own)
    stem_own = stem_tensors[0]
    with jax.named_scope("stem_other"):
        stem_other = swap(stem_own)
    own_later, sibling_later = lax.optimization_barrier((own, sibling))[:2]
    with jax.named_scope("side_far"):
        side_far = along_x(sibling_later)
    with jax.named_scope("turned"):
        turned = along_y(own_later)
    product = call(pair_kernel, matrix, [smem(), vmem(), vmem()],
                   [pltpu.VMEM((2, 2, BOND, BOND), BF16)], 2**28, 2**20)(after(where, sibling), stem_own, stem_other)
    with jax.named_scope("side_turned"):
        side_turned = along_y(after(side, product, turned))
    with jax.named_scope("across"):
        across = along_x(after(side, product, turned))
    with jax.named_scope("near"):
        near = along_z(product)
    with jax.named_scope("opposite"):
        opposite = across_z(product)
    with jax.named_scope("near_other"):
        near_other = swap(near)
    with jax.named_scope("side_far_turned"):
        side_far_turned = along_y(after(side_far, product))
    with jax.named_scope("across_turned"):
        across_turned = along_x(side_turned)
    ring = (product, near, near_other, opposite)
    total = call(ring_kernel, matrix, [smem()] + [vmem()] * 4,
                 [pltpu.VMEM((4, 2, BOND, BOND), BF16)], 2**29, 2**20)(where, *ring)
    with jax.named_scope("far"):
        far = across_y(total)
    hbm = pl.BlockSpec(memory_space=pltpu.HBM)
    parents = jnp.concatenate([first_parent.reshape(1, ROWS), second_parent.reshape(1, ROWS)], axis=0)
    x1, goes, place, table = call(
        prepare_kernel,
        (
            jax.ShapeDtypeStruct((2, ROOM, BOND), BF16),
            jax.ShapeDtypeStruct((8, SORTED), jnp.int32),
            jax.ShapeDtypeStruct((8, ROWS), F32),
            jax.ShapeDtypeStruct((8, NODES), jnp.int32),
        ),
        [smem(), vmem(), hbm],
        [
            pltpu.VMEM((SORTED, ROWS), BF16),
            pltpu.VMEM((ROWS, 2, BOND), BF16),
            pltpu.SemaphoreType.DMA,
        ],
        2**31, 2**22,
    )(after(where, total, across), parents, branch_rows)
    to2, back = call(
        select_kernel,
        (jax.ShapeDtypeStruct((SORTED, SORTED), BF16), jax.ShapeDtypeStruct((ROWS, SORTED), BF16)),
        [vmem(), vmem()], [], 2**30, 2**22,
    )(after(goes, side_turned), place)
    ends = call(ends_kernel, jax.ShapeDtypeStruct((2, 2, BOND, BOND), BF16), [smem()] + [vmem()] * 4,
                [pltpu.VMEM((4, 2, BOND, BOND), BF16)], 2**29, 2**20)(after(where, table), *ring)

    side_shared = shared(after(side, table))
    turned_shared = shared(after(turned, table))
    side_far_shared = shared(after(side_far, table))
    side_turned_shared = shared(after(side_turned, table))
    across_shared = shared(after(across, table))
    side_far_turned_shared = shared(after(side_far_turned, table))
    across_turned_shared = shared(after(across_turned, to2, ends))
    pairs = (
        (own, sibling), (side, side_shared), (turned, turned_shared), (side_far, side_far_shared),
        (side_turned, side_turned_shared), (across, across_shared),
        (side_far_turned, side_far_turned_shared), (across_turned, across_turned_shared),
    )
    slots = [value for pair in pairs for value in pair]

    second = call(
        nodes_kernel,
        jax.ShapeDtypeStruct((2, ROOM, BOND), BF16),
        [smem()] + [vmem()] * (2 + NODES),
        [pltpu.VMEM((2, ROOM, BOND), BF16)] * 2,
        2**33, 2**24,
    )(table, x1, to2, *slots)
    return call(
        stem_kernel, jax.ShapeDtypeStruct((ROWS, 2, BOND), BF16), [vmem()] * 4, [], 2**32, 2**23
    )(second, back, ends, after(far, second))


def solution(mesh):
    return jax.shard_map(
        body,
        mesh=mesh,
        in_specs=(
            P(AXES, None, None),
            P(AXES, None),
            P(AXES, None),
            P(("leaf", "slab"), None, None, None),
            P(("leaf", "slab"), None, None, None),
            P("stem", None, None, "slab", None),
        ),
        out_specs=P(AXES, None, None),
        check_vma=False,
    )
```
